512 devices in a mesh: date: 32 (over z_hi, y, core), strip: 16 (over x, z_lo).
Axes of the slice: x: 4, y: 8, z: 8 (z_hi: 2, z_lo: 4; z = z_hi * 4 + z_lo), core: 2. Of those that a mesh axis runs over, the one named last changes fastest.
Arguments:
- slc: bfloat16 [2, 64, 512, 1024], P(None, 'date', 'strip')
- block_order: int32 [32], replicated, may hold values from 0 to 31, each once
- az_offset: int32 [128], P('strip'), may hold values from 0 to 3
- rg_offset: int32 [256], replicated, may hold values from 0 to 3
Outputs:
- coherence: float32 [2, 64, 64, 128, 256], P(None, 'date', None, 'strip')
The draws below stay inside these ranges and needn't reach their ends.
Inputs may be any that keep to these rules, and one draw needn't show every extreme that they name: block_order is a permutation of the 32 chronological block numbers.
All inputs are finite; a program needn't handle non-finite values.
Results may differ from the reference program's by a relative error of at most 0.0003.
Values may be sent and summed in bfloat16 or wider, within the bound.
A program may use at most 64 MiB of HBM per device.

```python
import jax
import jax.numpy as jnp
from jax import lax

DATE_DEV = 2
RANGE = 1024
RG_WIN = 5
STEP = 4
HALO = 5
DATES = 64
BLOCKS = 32
LINES = 512
OUT_AZ = 128
OUT_RG = 256


def draw_slc(key, part):
    subkeys = jax.random.split(key, 6)
    scene_field = jax.random.normal(subkeys[0], (2, 1, LINES, RANGE), jnp.float32)
    phase_angle = jax.random.uniform(subkeys[1], (1, DATES, 1, 1), jnp.float32, -3.14159, 3.14159)
    roughness = jax.random.uniform(subkeys[5], (1, DATES, LINES, RANGE), jnp.float32, 0.5, 1.5)
    weight = jax.random.uniform(subkeys[2], (1, DATES, 1, 1), jnp.float32, 0.4, 1.2)
    noise_part = 0.7 * jax.random.normal(subkeys[4], (2, DATES, LINES, RANGE), jnp.float32)
    phase_cos = jnp.cos(phase_angle)
    phase_sin = jnp.sin(phase_angle)
    real_part = scene_field[0:1] * phase_cos - scene_field[1:2] * phase_sin
    imag_part = scene_field[0:1] * phase_sin + scene_field[1:2] * phase_cos
    signal = jnp.concatenate([real_part, imag_part], 0) * (weight * roughness)
    return (signal + noise_part).astype(jnp.bfloat16)


def plant(values, own_key, least, largest):
    extent = values.shape
    index_at = [jax.random.randint(jax.random.fold_in(own_key, axis), (), 0, extent[axis]) for axis in range(len(extent))]
    values = values.at[tuple(index_at)].set(least)
    longest = extent.index(max(extent))
    index_at[longest] = (index_at[longest] + 1) % extent[longest]
    return values.at[tuple(index_at)].set(largest)


def setup_inputs(seed: int = 0) -> dict:
    arg_keys = jax.random.split(jax.random.key(seed), 5)
    slc = draw_slc(jax.random.fold_in(arg_keys[4], 71), 0)
    block_order = jax.random.permutation(arg_keys[1], BLOCKS).astype(jnp.int32)
    az_offset = plant(jax.random.randint(arg_keys[2], (OUT_AZ,), 0, STEP), jax.random.fold_in(arg_keys[2], 1), 0, STEP - 1).astype(jnp.int32)
    rg_offset = plant(jax.random.randint(arg_keys[3], (OUT_RG,), 0, STEP), jax.random.fold_in(arg_keys[3], 1), 0, STEP - 1).astype(jnp.int32)
    return {"slc": slc, "block_order": block_order, "az_offset": az_offset, "rg_offset": rg_offset}


epsilon = 1e-06

def window_sums(field, az_box, rg_box):
    along = jnp.einsum('ol,...lr->...or', az_box, field, precision=lax.Precision.HIGHEST)
    return jnp.einsum('...or,rc->...oc', along, rg_box, precision=lax.Precision.HIGHEST)

def reference(slc, block_order, az_offset, rg_offset):
    data = slc.astype(jnp.float32)
    row_index = jnp.arange(OUT_AZ, dtype=jnp.int32)[:, None]
    lower = STEP * row_index + az_offset[:, None] - HALO
    line_index = jnp.arange(LINES, dtype=jnp.int32)[None]
    az_box = ((line_index >= lower) & (line_index <= lower + 2 * HALO)).astype(jnp.float32)
    centre = STEP * jnp.arange(OUT_RG, dtype=jnp.int32)[None] + rg_offset[None]
    sample = jnp.arange(RANGE, dtype=jnp.int32)[:, None]
    rg_box = (jnp.abs(sample - centre) <= RG_WIN // 2).astype(jnp.float32)
    scales = lax.rsqrt(window_sums(data[0] * data[0] + data[1] * data[1], az_box, rg_box) + epsilon)
    date_rank = (block_order[:, None] * DATE_DEV + jnp.arange(DATE_DEV, dtype=jnp.int32)[None]).reshape(-1)

    def one_row(inputs):
        single, own_scale, own_rank = inputs
        real_part = single[0] * data[0] + single[1] * data[1]
        imag_part = single[1] * data[0] - single[0] * data[1]
        sums = window_sums(jnp.stack([real_part, imag_part]), az_box, rg_box)
        coherent = sums * own_scale * scales[None]
        return jnp.where((date_rank > own_rank)[None, :, None, None], coherent, 0.0)
    all_rows = lax.map(one_row, (jnp.moveaxis(data, 1, 0), scales, date_rank))
    return jnp.moveaxis(all_rows, 0, 1)
```

```python
import functools

import jax
import jax.numpy as jnp
from jax import lax
from jax.experimental import pallas as pl
from jax.experimental.pallas import tpu as pltpu
from jax.sharding import PartitionSpec as P

RG_WIN = 5
STEP = 4
HALO = 5
EPSILON = 1e-06
MESH = pl.DeviceIdType.MESH

CHUNKS = 8
COLUMN = 8

BLOCKS = [
    (0, 0, 0, 0), (0, 0, 0, 1),
    (0, 0, 1, 0), (0, 1, 1, 0), (0, 0, 1, 1), (0, 1, 1, 1),
    (0, 0, 2, 0), (0, 1, 2, 0), (0, 0, 2, 1), (0, 1, 2, 1),
    (1, 0, 0, 0), (1, 0, 0, 1),
    (0, 0, 3, 0), (0, 1, 3, 0), (0, 0, 3, 1), (0, 1, 3, 1),
    (1, 0, 1, 0), (1, 1, 1, 0), (1, 0, 1, 1), (1, 1, 1, 1),
    (0, 0, 4, 0), (0, 0, 4, 1),
    (1, 0, 2, 0), (1, 1, 2, 0), (1, 0, 2, 1), (1, 1, 2, 1),
    (1, 0, 3, 0), (1, 1, 3, 0), (1, 0, 3, 1), (1, 1, 3, 1),
    (1, 0, 4, 0), (1, 0, 4, 1),
]
SLOT = {block: place for place, block in enumerate(BLOCKS)}
EVENTS = {
    1: [("ring", 0, 1, 0)],
    2: [("ring", 0, 1, 1)],
    4: [("across", 0)],
    6: [("ring", 0, 2, 0), ("ring", 0, 2, 1)],
    8: [("across", 1)],
    10: [("ring", 1, 1, 0)],
    12: [("ring", 0, 3, 0), ("ring", 0, 3, 1)],
    14: [("ring", 1, 1, 1)],
    16: [("ring", 1, 2, 0)],
    20: [("ring", 0, 4, 0)],
    22: [("ring", 1, 2, 1)],
    24: [("ring", 1, 3, 0)],
    26: [("ring", 1, 3, 1)],
    30: [("ring", 1, 4, 0)],
}


def slot_of(row, direction, distance, sibling=0):
    return SLOT[(row, direction if 0 < distance < 4 else 0, distance, sibling)]


def body(
    order, az_offset, rg_offset, x, out,
    held, own, fields, sums, box, scale,
    ring_send, ring_recv, halo_send, halo_recv, across_send, across_recv,
    sib_send, sib_recv, edge_send, edge_recv, local_sem,
):
    date, strip = lax.axis_index("date"), lax.axis_index("strip")
    strips = lax.axis_size("strip")
    core, y, half = date % 2, (date // 2) % COLUMN, date // (2 * COLUMN)
    lines = x.shape[2]
    total = held.shape[3]

    def at(half_, y_, core_):
        return half_ * (2 * COLUMN) + ((y_ + COLUMN) % COLUMN) * 2 + core_

    upper, lower = (at(half, y + 1, core), strip), (at(half, y - 1, core), strip)
    facing, sibling = (at(1 - half, y, core), strip), (at(half, y, 1 - core), strip)
    after = (date, (strip + 1) % strips)
    before = (date, (strip + strips - 1) % strips)

    barrier = pltpu.get_barrier_semaphore()
    for target in (upper, lower, facing, sibling, after, before):
        pl.semaphore_signal(barrier, inc=1, device_id=target, device_id_type=MESH)
    pl.semaphore_wait(barrier, 6)

    def copy(src, dst, send, recv, target):
        return pltpu.make_async_remote_copy(
            src_ref=src, dst_ref=dst, send_sem=send, recv_sem=recv, device_id=target, device_id_type=MESH
        )

    def to_after():
        return copy(
            x.at[:, :, pl.ds(lines - HALO, HALO)], held.at[0, :, :, pl.ds(lines, HALO)],
            edge_send.at[0], edge_recv.at[0], after,
        )

    def to_before():
        return copy(
            x.at[:, :, pl.ds(0, HALO)], held.at[0, :, :, pl.ds(lines + HALO, HALO)],
            edge_send.at[1], edge_recv.at[1], before,
        )

    def ring(row, direction, distance, part):
        target = upper if direction == 0 else lower
        place = slot_of(row, direction, distance)
        index = (row, direction, distance - 1, part)
        send, recv = ring_send.at[index], ring_recv.at[index]
        if row == 0 and distance == 1 and part == 0:
            main = pl.ds(0, lines)
            return copy(x.at[0], held.at[place, 0, :, main], send, recv, target)
        source = slot_of(row, direction, distance - 1)
        return copy(held.at[source, part], held.at[place, part], send, recv, target)

    def ring_halo(direction):
        target = upper if direction == 0 else lower
        edge = pl.ds(lines, 2 * HALO)
        return copy(
            held.at[0, 0, :, edge], held.at[slot_of(0, direction, 1), 0, :, edge],
            halo_send.at[direction], halo_recv.at[direction], target,
        )

    def across(part):
        place = slot_of(1, 0, 0)
        send, recv = across_send.at[part], across_recv.at[part]
        if part == 0:
            return copy(x.at[0], held.at[place, 0, :, pl.ds(0, lines)], send, recv, facing)
        return copy(held.at[0, 1], held.at[place, 1], send, recv, facing)

    def across_halo():
        edge = pl.ds(lines, 2 * HALO)
        return copy(
            held.at[0, 0, :, edge], held.at[slot_of(1, 0, 0), 0, :, edge],
            halo_send.at[2], halo_recv.at[2], facing,
        )

    def beside(row, direction, distance, part):
        source, place = slot_of(row, direction, distance), slot_of(row, direction, distance, 1)
        send, recv = sib_send.at[place, part], sib_recv.at[place, part]
        if source == 0 and part == 0:
            return copy(x.at[0], held.at[place, 0, :, pl.ds(0, lines)], send, recv, sibling)
        return copy(held.at[source, part], held.at[place, part], send, recv, sibling)

    def beside_halo():
        edge = pl.ds(lines, 2 * HALO)
        return copy(
            held.at[0, 0, :, edge], held.at[1, 0, :, edge], halo_send.at[3], halo_recv.at[3], sibling
        )

    def parts_of(direction, distance):
        return (0, 1) if distance < 4 else (direction,)

    def start_ring(row, distance, part):
        for direction in (0, 1):
            if part in parts_of(direction, distance):
                ring(row, direction, distance, part).start()

    def event(kind, *what):
        if kind == "across":
            (part,) = what
            across(part).wait_recv()
            if part == 0:
                across_halo().wait_recv()
            start_ring(1, 1, part)
            beside(1, 0, 0, part).start()
            return
        row, distance, part = what
        for direction in (0, 1):
            if distance == 4:
                part = direction
            ring(row, direction, distance, part).wait_recv()
            if row == 0 and distance == 1 and part == 0:
                ring_halo(direction).wait_recv()
            if distance < 4 and part in parts_of(direction, distance + 1):
                ring(row, direction, distance + 1, part).start()
            beside(row, direction, distance, part).start()

    to_after().start()
    to_before().start()
    local = pltpu.make_async_copy(x, held.at[0, :, :, pl.ds(0, lines)], local_sem)
    local.start()
    across(0).start()
    start_ring(0, 1, 0)
    beside(0, 0, 0, 0).start()

    columns = box.shape[1]
    sample = lax.broadcasted_iota(jnp.int32, (128, columns), 0)
    centre = STEP * lax.broadcasted_iota(jnp.int32, (128, columns), 1) + rg_offset[...]
    for chunk in range(CHUNKS):
        inside = jnp.abs(sample + 128 * chunk - centre) <= RG_WIN // 2
        box[pl.ds(128 * chunk, 128), :] = jnp.where(inside, 1.0, 0.0).astype(jnp.bfloat16)

    local.wait()
    to_after().wait_recv()
    to_before().wait_recv()

    @pl.when(strip == 0)
    def _():
        held[0, :, :, lines : lines + HALO] = jnp.zeros((2, 2, HALO, CHUNKS, 128), held.dtype)

    @pl.when(strip == strips - 1)
    def _():
        held[0, :, :, lines + HALO :] = jnp.zeros((2, 2, HALO, CHUNKS, 128), held.dtype)

    across_halo().start()
    for direction in (0, 1):
        ring_halo(direction).start()
    beside_halo().start()
    across(1).start()
    start_ring(0, 1, 1)
    beside(0, 0, 0, 1).start()

    for part in (0, 1):
        for mine in (0, 1):
            own[part, mine] = held[0, part, mine].astype(jnp.float32)

    spans = [(first, 4, first + HALO) for first in range(0, lines, 4)]
    spans += [(lines, HALO, 0), (lines + HALO, HALO, lines + HALO)]

    def work(step, carry):
        for place, events in EVENTS.items():

            @pl.when(step == place)
            def _():
                for one in events:
                    event(*one)

        for place, (row, direction, distance, side) in enumerate(BLOCKS):
            if side:

                @pl.when(step == place)
                def _():
                    parts = (0, 1)
                    for part in parts:
                        beside(row, direction, distance, part).wait_recv()
                    if place == 1:
                        beside_halo().wait_recv()

        block = 0
        for place, (row, direction, distance, side) in enumerate(BLOCKS):
            y_ = y - distance if direction == 0 else y + distance
            index = at(1 - half if row else half, y_, 1 - core if side else core)
            block = jnp.where(step == place, index, block)

        def one_date(other, inner):
            for first, count, place in spans:
                here = pl.ds(first, count)
                there = pl.ds(place, count)
                b_re = held[step, 0, other, here].astype(jnp.float32)
                b_im = held[step, 1, other, here].astype(jnp.float32)
                for mine in (0, 1):
                    a_re, a_im = own[0, mine, here], own[1, mine, here]
                    fields[2 * mine, there] = a_re * b_re + a_im * b_im
                    fields[2 * mine + 1, there] = a_im * b_re - a_re * b_im
                fields[4, there] = b_re * b_re + b_im * b_im
            for o in range(lines // STEP):
                start = az_offset[o] + STEP * o
                for f in range(5):
                    window = jnp.sum(fields[f, pl.ds(start, 2 * HALO + 1)], axis=0)
                    sums[pl.ds(pl.multiple_of(other * 320 + f * 64 + o * 8, 8), 8), :] = window
            return inner

        lax.fori_loop(0, 2, one_date, 0)
        wide = jnp.concatenate([sums[pl.ds(chunk, 80, stride=CHUNKS), :] for chunk in range(CHUNKS)], axis=1)
        high = wide.astype(jnp.bfloat16)
        low = (wide - high.astype(jnp.float32)).astype(jnp.bfloat16)
        both = jnp.dot(jnp.concatenate([high, low], axis=0), box[...], preferred_element_type=jnp.float32)
        cross = both[:80] + both[80:]
        others = [lax.rsqrt(cross[40 * other + 32 : 40 * other + 40] + EPSILON) for other in (0, 1)]

        @pl.when(step == 0)
        def _():
            for mine in (0, 1):
                scale[mine] = others[mine]

        for mine in (0, 1):
            mine_scale = scale[mine]
            for other in (0, 1):
                later = order[block] * 2 + other > order[date] * 2 + mine
                for part in (0, 1):
                    first = 40 * other + 16 * mine + 8 * part
                    value = cross[first : first + 8] * mine_scale * others[other]
                    out[part, mine, block * 2 + other] = jnp.where(later, value, 0.0)
        return carry

    lax.fori_loop(0, len(BLOCKS), work, 0)

    to_after().wait_send()
    to_before().wait_send()
    for direction in (0, 1):
        ring_halo(direction).wait_send()
        for row in (0, 1):
            for distance in (1, 2, 3, 4):
                for part in parts_of(direction, distance):
                    ring(row, direction, distance, part).wait_send()
                    beside(row, direction, distance, part).wait_send()
    across_halo().wait_send()
    beside_halo().wait_send()
    for part in (0, 1):
        across(part).wait_send()
        for row in (0, 1):
            beside(row, 0, 0, part).wait_send()


def on_device(slc, block_order, az_offset, rg_offset):
    parts, dates, lines, samples = slc.shape
    rows, columns = lines // STEP, samples // STEP
    count = block_order.shape[0]
    total = lines + 2 * HALO
    vmem = pl.BlockSpec(memory_space=pltpu.VMEM)
    smem = pl.BlockSpec(memory_space=pltpu.SMEM)
    dma = pltpu.SemaphoreType.DMA
    return pl.pallas_call(
        body,
        out_shape=jax.ShapeDtypeStruct((2, dates, dates * count, rows, columns), jnp.float32),
        in_specs=[smem, smem, vmem, vmem],
        out_specs=vmem,
        scratch_shapes=[
            pltpu.VMEM((count, 2, dates, total, CHUNKS, 128), jnp.bfloat16),
            pltpu.VMEM((2, dates, total, CHUNKS, 128), jnp.float32),
            pltpu.VMEM((5, total, CHUNKS, 128), jnp.float32),
            pltpu.VMEM((2 * 5 * rows * CHUNKS, 128), jnp.float32),
            pltpu.VMEM((samples, columns), jnp.bfloat16),
            pltpu.VMEM((dates, rows, columns), jnp.float32),
            dma((2, 2, 4, 2)), dma((2, 2, 4, 2)),
            dma((4,)), dma((4,)),
            dma((2,)), dma((2,)),
            dma((count, 2)), dma((count, 2)),
            dma((2,)), dma((2,)),
            dma,
        ],
        compiler_params=pltpu.CompilerParams(
            collective_id=0, has_side_effects=True, vmem_limit_bytes=48 * 2**20
        ),
    )(block_order, az_offset, rg_offset[None], slc.reshape(parts, dates, lines, CHUNKS, 128))


def solution(mesh):
    placed = (P(None, "date", "strip", None), P(), P("strip"), P())
    return jax.shard_map(
        on_device,
        mesh=mesh,
        in_specs=placed,
        out_specs=P(None, "date", None, "strip", None),
        check_vma=False,
    )
```

```python
import functools

import jax
import jax.numpy as jnp
from jax import lax
from jax.experimental import pallas as pl
from jax.experimental.pallas import tpu as pltpu
from jax.sharding import PartitionSpec as P

RG_WIN = 5
STEP = 4
HALO = 5
EPSILON = 1e-06
MESH = pl.DeviceIdType.MESH

CHUNKS = 8
COLUMN = 8

BLOCKS = [
    (0, 0, 0, 0), (0, 0, 0, 1),
    (0, 0, 1, 0), (0, 1, 1, 0), (0, 0, 1, 1), (0, 1, 1, 1),
    (0, 0, 2, 0), (0, 1, 2, 0), (0, 0, 2, 1), (0, 1, 2, 1),
    (1, 0, 0, 0), (1, 0, 0, 1),
    (0, 0, 3, 0), (0, 1, 3, 0), (0, 0, 3, 1), (0, 1, 3, 1),
    (1, 0, 1, 0), (1, 1, 1, 0), (1, 0, 1, 1), (1, 1, 1, 1),
    (0, 0, 4, 0), (0, 0, 4, 1),
    (1, 0, 2, 0), (1, 1, 2, 0), (1, 0, 2, 1), (1, 1, 2, 1),
    (1, 0, 3, 0), (1, 1, 3, 0), (1, 0, 3, 1), (1, 1, 3, 1),
    (1, 0, 4, 0), (1, 0, 4, 1),
]
SLOT = {block: place for place, block in enumerate(BLOCKS)}
FIRST = -2
LAG = 10
EVENTS = {
    -2: [("ring", 0, 1, 0)],
    -1: [("ring", 0, 1, 1)],
    0: [("offsets",)],
    2: [("across", 0)],
    3: [("ring", 0, 2, 0)],
    4: [("ring", 0, 2, 1)],
    6: [("across", 1)],
    8: [("ring", 1, 1, 0)],
    10: [("ring", 0, 3, 0)],
    12: [("ring", 0, 3, 1)],
    14: [("ring", 1, 1, 1)],
    16: [("ring", 1, 2, 0)],
    19: [("ring", 0, 4, 0)],
    21: [("ring", 1, 2, 1)],
    24: [("ring", 1, 3, 0)],
    26: [("ring", 1, 3, 1)],
    30: [("ring", 1, 4, 0)],
}
for place, (row, direction, distance, sibling) in enumerate(BLOCKS):
    if sibling:
        EVENTS.setdefault(place, []).append(("beside", row, direction, distance))


def slot_of(row, direction, distance, sibling=0):
    return SLOT[(row, direction if 0 < distance < 4 else 0, distance, sibling)]


def picked(place, values):
    while len(values) > 1:
        odd = place % 2 == 1
        values = [jnp.where(odd, high, low) for low, high in zip(values[::2], values[1::2])]
        place = place // 2
    return values[0]


def body(
    small, x, out,
    held, own, fields, sums, box, scale, cross, from_before, from_after,
    numbers, my_offsets, next_offsets, last_offsets,
    ring_send, ring_recv, across_send, across_recv, sib_send, sib_recv, offset_send, offset_recv,
    part_send, part_recv, local_sem,
):
    date, strip = lax.axis_index("date"), lax.axis_index("strip")
    strips = lax.axis_size("strip")
    core, y, half = date % 2, (date // 2) % COLUMN, date // (2 * COLUMN)
    lines = x.shape[2]
    rows, columns = lines // STEP, box.shape[1]
    first_az = columns + len(BLOCKS)

    def at(half_, y_, core_):
        return half_ * (2 * COLUMN) + ((y_ + COLUMN) % COLUMN) * 2 + core_

    upper, lower = (at(half, y + 1, core), strip), (at(half, y - 1, core), strip)
    facing, sibling = (at(1 - half, y, core), strip), (at(half, y, 1 - core), strip)
    after = (date, (strip + 1) % strips)
    before = (date, (strip + strips - 1) % strips)

    to_scalars = pltpu.make_async_copy(small, numbers, local_sem.at[1])
    to_scalars.start()
    barrier = pltpu.get_barrier_semaphore()
    for target in (upper, lower, facing, sibling, after, before):
        pl.semaphore_signal(barrier, inc=1, device_id=target, device_id_type=MESH)
    pl.semaphore_wait(barrier, 6)

    def copy(src, dst, send, recv, target):
        return pltpu.make_async_remote_copy(
            src_ref=src, dst_ref=dst, send_sem=send, recv_sem=recv, device_id=target, device_id_type=MESH
        )

    def offset(which):
        send, recv = offset_send.at[which], offset_recv.at[which]
        if which == 0:
            return copy(my_offsets.at[pl.ds(2, 2)], last_offsets, send, recv, after)
        return copy(my_offsets.at[pl.ds(0, 2)], next_offsets, send, recv, before)

    def source_of(row, direction, distance, part):
        if row == 0 and distance == 0:
            return x.at[part]
        return held.at[slot_of(row, direction, distance), part]

    def ring(row, direction, distance, part):
        target = upper if direction == 0 else lower
        index = (row, direction, distance - 1, part)
        return copy(
            source_of(row, direction, distance - 1, part), held.at[slot_of(row, direction, distance), part],
            ring_send.at[index], ring_recv.at[index], target,
        )

    def across(part):
        return copy(
            x.at[part], held.at[slot_of(1, 0, 0), part], across_send.at[part], across_recv.at[part], facing
        )

    def beside(row, direction, distance, part):
        place = slot_of(row, direction, distance, 1)
        return copy(
            source_of(row, direction, distance, part), held.at[place, part],
            sib_send.at[place, part], sib_recv.at[place, part], sibling,
        )

    def to_after(place):
        return copy(
            cross.at[place, pl.ds(80, 24)], from_before.at[place], part_send.at[0, place], part_recv.at[0, place],
            after,
        )

    def to_before(place):
        return copy(
            cross.at[place, pl.ds(104, 24)], from_after.at[place], part_send.at[1, place], part_recv.at[1, place],
            before,
        )

    def parts_of(direction, distance):
        return (0, 1) if distance < 4 else (direction,)

    local = pltpu.make_async_copy(x, held.at[0], local_sem.at[0])

    def event(kind, *what):
        if kind == "offsets":
            offset(0).wait_recv()
            offset(1).wait_recv()
            local.wait()
        elif kind == "across":
            (part,) = what
            across(part).wait_recv()
            for direction in (0, 1):
                ring(1, direction, 1, part).start()
            beside(1, 0, 0, part).start()
        elif kind == "ring":
            row, distance, part = what
            for direction in (0, 1):
                if distance == 4:
                    part = direction
                ring(row, direction, distance, part).wait_recv()
                if distance < 4 and part in parts_of(direction, distance + 1):
                    ring(row, direction, distance + 1, part).start()
                beside(row, direction, distance, part).start()
        else:
            for part in (0, 1):
                beside(*what, part).wait_recv()

    for part in (0, 1):
        across(part).start()
        for direction in (0, 1):
            ring(0, direction, 1, part).start()
    local.start()
    for part in (0, 1):
        beside(0, 0, 0, part).start()
    to_scalars.wait()

    def az_offset(o):
        return numbers[0, first_az + o]

    for which, o in enumerate((0, 1, rows - 2, rows - 1)):
        my_offsets[which] = jnp.full((8, 128), az_offset(o), jnp.int32).astype(jnp.float32)
    offset(0).start()
    offset(1).start()

    sample = lax.broadcasted_iota(jnp.int32, (128, columns), 0)
    centre = STEP * lax.broadcasted_iota(jnp.int32, (128, columns), 1) + small[:, :columns]
    for chunk in range(CHUNKS):
        inside = jnp.abs(sample + 128 * chunk - centre) <= RG_WIN // 2
        box[pl.ds(128 * chunk, 128), :] = jnp.where(inside, 1.0, 0.0).astype(jnp.bfloat16)
    nothing = jnp.zeros((HALO, CHUNKS, 128), jnp.float32)
    for f in range(5):
        fields[f, 0:HALO] = nothing
        fields[f, lines + HALO :] = nothing
    sums[80 * 8 :, :] = jnp.zeros((48 * 8, 128), jnp.float32)
    for part in (0, 1):
        for mine in (0, 1):
            own[part, mine] = x[part, mine].astype(jnp.float32)

    def steps(step, low, high):
        here = [place for place in EVENTS if low <= place < high]
        if high - low == 1 or not here:
            for place in here:
                for one in EVENTS[place]:
                    event(*one)
            return
        middle = (low + high) // 2

        @pl.when(step < middle)
        def _():
            steps(step, low, middle)

        @pl.when(step >= middle)
        def _():
            steps(step, middle, high)

    def one_step(step, carry):
        @pl.when(step < len(BLOCKS))
        def _():
            steps(step, FIRST, len(BLOCKS))

        @pl.when(jnp.logical_and(step >= 0, step < len(BLOCKS)))
        def _():
            own_sums(step)

        @pl.when(step >= LAG)
        def _():
            finish(step - LAG)

        return carry

    def own_sums(place):
        def one_date(other, inner):
            for first in range(0, lines, 4):
                here, there = pl.ds(first, 4), pl.ds(first + HALO, 4)
                b_re = held[place, 0, other, here].astype(jnp.float32)
                b_im = held[place, 1, other, here].astype(jnp.float32)
                for mine in (0, 1):
                    a_re, a_im = own[0, mine, here], own[1, mine, here]
                    fields[2 * mine, there] = a_re * b_re + a_im * b_im
                    fields[2 * mine + 1, there] = a_im * b_re - a_re * b_im
                fields[4, there] = b_re * b_re + b_im * b_im
            for o in range(rows):
                start = az_offset(o) + STEP * o
                for f in range(5):
                    window = jnp.sum(fields[f, pl.ds(start, 2 * HALO + 1)], axis=0)
                    sums[pl.ds(pl.multiple_of(other * 320 + f * 64 + o * 8, 8), 8), :] = window
            ahead, ahead_second = next_offsets[0], next_offsets[1]
            sixth, seventh = last_offsets[0], last_offsets[1]
            for f in range(5):
                line = [fields[f, HALO + l] for l in range(HALO)]
                near = line[0] + line[1]
                for l in (2, 3, 4):
                    near = near + jnp.where(seventh >= l - 1, line[l], 0.0)
                single = jnp.where(sixth >= 3, line[0], 0.0)
                line = [fields[f, lines + l] for l in range(HALO)]
                far = line[3] + line[4]
                for l in (0, 1, 2):
                    far = far + jnp.where(ahead <= l, line[l], 0.0)
                far_second = jnp.where(ahead_second <= 0, line[4], 0.0)
                for group, value in ((80, far), (90, far_second), (104, single), (114, near)):
                    sums[pl.ds(pl.multiple_of((group + other * 5 + f) * 8, 8), 8), :] = value
            return inner

        lax.fori_loop(0, 2, one_date, 0)
        wide = jnp.concatenate([sums[pl.ds(chunk, 128, stride=CHUNKS), :] for chunk in range(CHUNKS)], axis=1)
        high = wide.astype(jnp.bfloat16)
        low = (wide - high.astype(jnp.float32)).astype(jnp.bfloat16)
        both = jnp.dot(jnp.concatenate([high, low], axis=0), box[...], preferred_element_type=jnp.float32)
        cross[place] = both[:128] + both[128:]
        to_after(place).start()
        to_before(place).start()

    sub = lax.broadcasted_iota(jnp.int32, (rows, columns), 0)
    top = jnp.logical_and(sub == 0, strip > 0)
    second = jnp.logical_and(sub == 1, strip > 0)
    next_last = jnp.logical_and(sub == rows - 2, strip < strips - 1)
    last = jnp.logical_and(sub == rows - 1, strip < strips - 1)
    indices = []
    for row, direction, distance, side in BLOCKS:
        y_ = y - distance if direction == 0 else y + distance
        indices.append(at(1 - half if row else half, y_, 1 - core if side else core))

    def finish(place):
        block = picked(place, indices)
        to_after(place).wait_recv()
        to_before(place).wait_recv()

        def whole(f):
            value = cross[place, 8 * f : 8 * f + 8]
            value = value + jnp.where(top, from_before[place, f : f + 1], 0.0)
            value = value + jnp.where(second, from_before[place, 10 + f : 11 + f], 0.0)
            value = value + jnp.where(next_last, from_after[place, f : f + 1], 0.0)
            return value + jnp.where(last, from_after[place, 10 + f : 11 + f], 0.0)

        others = [lax.rsqrt(whole(5 * other + 4) + EPSILON) for other in (0, 1)]

        @pl.when(place == 0)
        def _():
            for mine in (0, 1):
                scale[mine] = others[mine]

        for mine in (0, 1):
            mine_scale = scale[mine]
            for other in (0, 1):
                later = numbers[0, columns + block] * 2 + other > numbers[0, columns + date] * 2 + mine
                for part in (0, 1):
                    value = whole(5 * other + 2 * mine + part) * mine_scale * others[other]
                    out[part, mine, block * 2 + other] = jnp.where(later, value, 0.0)

    lax.fori_loop(0, len(BLOCKS) + LAG - FIRST, lambda n, c: one_step(n + FIRST, c), 0)

    for which in (0, 1):
        offset(which).wait_send()
        across(which).wait_send()
    for row in (0, 1):
        for distance in range(5):
            for direction in (0, 1) if distance else (0,):
                for part in parts_of(direction, distance):
                    if distance:
                        ring(row, direction, distance, part).wait_send()
                    beside(row, direction, distance, part).wait_send()

    def sent(place, carry):
        to_after(place).wait_send()
        to_before(place).wait_send()
        return carry

    lax.fori_loop(0, len(BLOCKS), sent, 0)


def on_device(slc, block_order, az_offset, rg_offset):
    parts, dates, lines, samples = slc.shape
    rows, columns = lines // STEP, samples // STEP
    count = block_order.shape[0]
    total = lines + 2 * HALO
    vmem = pl.BlockSpec(memory_space=pltpu.VMEM)
    dma = pltpu.SemaphoreType.DMA
    tile = (CHUNKS, 128)
    small = jnp.concatenate([rg_offset, block_order, az_offset])
    width = -(-small.shape[0] // 128) * 128
    small = jnp.pad(small, (0, width - small.shape[0]))[None]
    return pl.pallas_call(
        body,
        out_shape=jax.ShapeDtypeStruct((2, dates, dates * count, rows, columns), jnp.float32),
        in_specs=[vmem, vmem],
        out_specs=vmem,
        scratch_shapes=[
            pltpu.VMEM((count, 2, dates, lines, *tile), jnp.bfloat16),
            pltpu.VMEM((2, dates, lines, *tile), jnp.float32),
            pltpu.VMEM((5, total, *tile), jnp.float32),
            pltpu.VMEM((128 * CHUNKS, 128), jnp.float32),
            pltpu.VMEM((samples, columns), jnp.bfloat16),
            pltpu.VMEM((dates, rows, columns), jnp.float32),
            pltpu.VMEM((count, 128, columns), jnp.float32),
            pltpu.VMEM((count, 24, columns), jnp.float32),
            pltpu.VMEM((count, 24, columns), jnp.float32),
            pltpu.SMEM((1, width), jnp.int32),
            pltpu.VMEM((4, 8, 128), jnp.float32),
            pltpu.VMEM((2, 8, 128), jnp.float32),
            pltpu.VMEM((2, 8, 128), jnp.float32),
            dma((2, 2, 4, 2)), dma((2, 2, 4, 2)),
            dma((2,)), dma((2,)),
            dma((count, 2)), dma((count, 2)),
            dma((2,)), dma((2,)),
            dma((2, count)), dma((2, count)),
            dma((2,)),
        ],
        compiler_params=pltpu.CompilerParams(
            collective_id=0, has_side_effects=True, vmem_limit_bytes=48 * 2**20
        ),
    )(small, slc.reshape(parts, dates, lines, *tile))


def solution(mesh):
    placed = (P(None, "date", "strip", None), P(), P("strip"), P())
    return jax.shard_map(
        on_device,
        mesh=mesh,
        in_specs=placed,
        out_specs=P(None, "date", None, "strip", None),
        check_vma=False,
    )
```

```python
import functools

import jax
import jax.numpy as jnp
from jax import lax
from jax.experimental import pallas as pl
from jax.experimental.pallas import tpu as pltpu
from jax.sharding import PartitionSpec as P

RG_WIN = 5
STEP = 4
HALO = 5
EPSILON = 1e-06
MESH = pl.DeviceIdType.MESH

CHUNKS = 8
COLUMN = 8

BLOCKS = [
    (0, 0, 0, 0), (0, 0, 0, 1),
    (0, 0, 1, 0), (0, 1, 1, 0), (0, 0, 1, 1), (0, 1, 1, 1),
    (0, 0, 2, 0), (0, 1, 2, 0), (0, 0, 2, 1), (0, 1, 2, 1),
    (1, 0, 0, 0), (1, 0, 0, 1),
    (0, 0, 3, 0), (0, 1, 3, 0), (0, 0, 3, 1), (0, 1, 3, 1),
    (1, 0, 1, 0), (1, 1, 1, 0), (1, 0, 1, 1), (1, 1, 1, 1),
    (0, 0, 4, 0), (0, 0, 4, 1),
    (1, 0, 2, 0), (1, 1, 2, 0), (1, 0, 2, 1), (1, 1, 2, 1),
    (1, 0, 3, 0), (1, 1, 3, 0), (1, 0, 3, 1), (1, 1, 3, 1),
    (1, 0, 4, 0), (1, 0, 4, 1),
]
SLOT = {block: place for place, block in enumerate(BLOCKS)}
FIRST = -2
LAG = 10
EVENTS = {
    -2: [("ring", 0, 1, 0)],
    -1: [("ring", 0, 1, 1)],
    0: [("offsets",)],
    2: [("across", 0)],
    3: [("ring", 0, 2, 0)],
    4: [("ring", 0, 2, 1)],
    6: [("across", 1)],
    8: [("ring", 1, 1, 0)],
    10: [("ring", 0, 3, 0)],
    12: [("ring", 0, 3, 1)],
    14: [("ring", 1, 1, 1)],
    16: [("ring", 1, 2, 0)],
    19: [("ring", 0, 4, 0)],
    21: [("ring", 1, 2, 1)],
    24: [("ring", 1, 3, 0)],
    26: [("ring", 1, 3, 1)],
    30: [("ring", 1, 4, 0)],
}
for place, (row, direction, distance, sibling) in enumerate(BLOCKS):
    if sibling:
        EVENTS.setdefault(place, []).append(("beside", row, direction, distance))


def slot_of(row, direction, distance, sibling=0):
    return SLOT[(row, direction if 0 < distance < 4 else 0, distance, sibling)]


def picked(place, values):
    while len(values) > 1:
        odd = place % 2 == 1
        values = [jnp.where(odd, high, low) for low, high in zip(values[::2], values[1::2])]
        place = place // 2
    return values[0]


def body(
    small, x, out,
    held, own, fields, quads, sums, box, scale, cross, from_before, from_after,
    numbers, outer, my_offsets, next_offsets, last_offsets,
    ring_send, ring_recv, across_send, across_recv, sib_send, sib_recv, offset_send, offset_recv,
    part_send, part_recv, local_sem,
):
    date, strip = lax.axis_index("date"), lax.axis_index("strip")
    strips = lax.axis_size("strip")
    core, y, half = date % 2, (date // 2) % COLUMN, date // (2 * COLUMN)
    lines = x.shape[2]
    rows, columns = lines // STEP, box.shape[1]
    first_az = columns + len(BLOCKS)

    def at(half_, y_, core_):
        return half_ * (2 * COLUMN) + ((y_ + COLUMN) % COLUMN) * 2 + core_

    upper, lower = (at(half, y + 1, core), strip), (at(half, y - 1, core), strip)
    facing, sibling = (at(1 - half, y, core), strip), (at(half, y, 1 - core), strip)
    after = (date, (strip + 1) % strips)
    before = (date, (strip + strips - 1) % strips)

    to_scalars = pltpu.make_async_copy(small, numbers, local_sem.at[1])
    to_scalars.start()
    barrier = pltpu.get_barrier_semaphore()
    for target in (upper, lower, facing, sibling, after, before):
        pl.semaphore_signal(barrier, inc=1, device_id=target, device_id_type=MESH)
    pl.semaphore_wait(barrier, 6)

    def copy(src, dst, send, recv, target):
        return pltpu.make_async_remote_copy(
            src_ref=src, dst_ref=dst, send_sem=send, recv_sem=recv, device_id=target, device_id_type=MESH
        )

    def offset(which):
        send, recv = offset_send.at[which], offset_recv.at[which]
        if which == 0:
            return copy(my_offsets.at[pl.ds(2, 2)], last_offsets, send, recv, after)
        return copy(my_offsets.at[pl.ds(0, 2)], next_offsets, send, recv, before)

    def source_of(row, direction, distance, part):
        if row == 0 and distance == 0:
            return x.at[part]
        return held.at[slot_of(row, direction, distance), part]

    def ring(row, direction, distance, part):
        target = upper if direction == 0 else lower
        index = (row, direction, distance - 1, part)
        return copy(
            source_of(row, direction, distance - 1, part), held.at[slot_of(row, direction, distance), part],
            ring_send.at[index], ring_recv.at[index], target,
        )

    def across(part):
        return copy(
            x.at[part], held.at[slot_of(1, 0, 0), part], across_send.at[part], across_recv.at[part], facing
        )

    def beside(row, direction, distance):
        place = slot_of(row, direction, distance, 1)
        source = x if row == 0 and distance == 0 else held.at[slot_of(row, direction, distance)]
        return copy(source, held.at[place], sib_send.at[place], sib_recv.at[place], sibling)

    def to_after(place):
        return copy(
            cross.at[place, pl.ds(80, 24)], from_before.at[place], part_send.at[0, place], part_recv.at[0, place],
            after,
        )

    def to_before(place):
        return copy(
            cross.at[place, pl.ds(104, 24)], from_after.at[place], part_send.at[1, place], part_recv.at[1, place],
            before,
        )

    def parts_of(direction, distance):
        return (0, 1) if distance < 4 else (direction,)

    local = pltpu.make_async_copy(x, held.at[0], local_sem.at[0])

    def event(kind, *what):
        if kind == "offsets":
            offset(0).wait_recv()
            offset(1).wait_recv()
            local.wait()
        elif kind == "across":
            (part,) = what
            across(part).wait_recv()
            for direction in (0, 1):
                ring(1, direction, 1, part).start()
            if part == 1:
                beside(1, 0, 0).start()
        elif kind == "ring":
            row, distance, part = what
            for direction in (0, 1):
                if distance == 4:
                    part = direction
                ring(row, direction, distance, part).wait_recv()
                if distance < 4 and part in parts_of(direction, distance + 1):
                    ring(row, direction, distance + 1, part).start()
                if part == 1 and (distance < 4 or direction == 1):
                    beside(row, direction, distance).start()
        else:
            beside(*what).wait_recv()

    for part in (0, 1):
        across(part).start()
        for direction in (0, 1):
            ring(0, direction, 1, part).start()
    local.start()
    beside(0, 0, 0).start()
    to_scalars.wait()

    def az_offset(o):
        return numbers[0, first_az + o]

    for which, o in enumerate((0, 1, rows - 2, rows - 1)):
        my_offsets[which] = jnp.full((8, 128), az_offset(o), jnp.int32).astype(jnp.float32)
    offset(0).start()
    offset(1).start()

    sample = lax.broadcasted_iota(jnp.int32, (128, columns), 0)
    centre = STEP * lax.broadcasted_iota(jnp.int32, (128, columns), 1) + small[:, :columns]
    for chunk in range(CHUNKS):
        inside = jnp.abs(sample + 128 * chunk - centre) <= RG_WIN // 2
        box[pl.ds(128 * chunk, 128), :] = jnp.where(inside, 1.0, 0.0).astype(jnp.bfloat16)
    nothing = jnp.zeros((HALO, CHUNKS, 128), jnp.float32)
    for other in (0, 1):
        for f in range(5):
            fields[other, f, 0:HALO] = nothing
            fields[other, f, lines + HALO :] = nothing
    spans = [(0, 2)] + [(first, 4) for first in range(2, lines - 2, 4)] + [(lines - 2, 2)]
    for o in range(rows):
        for k in range(3):
            outer[3 * o + k] = STEP * o + k + jnp.where(az_offset(o) > k, 2 * HALO + 1, 0)
    sums[80 * 8 :, :] = jnp.zeros((48 * 8, 128), jnp.float32)
    for part in (0, 1):
        for mine in (0, 1):
            own[part, mine] = x[part, mine].astype(jnp.float32)

    def steps(step, low, high):
        here = [place for place in EVENTS if low <= place < high]
        if high - low == 1 or not here:
            for place in here:
                for one in EVENTS[place]:
                    event(*one)
            return
        middle = (low + high) // 2

        @pl.when(step < middle)
        def _():
            steps(step, low, middle)

        @pl.when(step >= middle)
        def _():
            steps(step, middle, high)

    def one_step(step, carry):
        @pl.when(step < len(BLOCKS))
        def _():
            steps(step, FIRST, len(BLOCKS))

        @pl.when(jnp.logical_and(step >= 0, step < len(BLOCKS)))
        def _():
            own_sums(step)

        @pl.when(step >= LAG)
        def _():
            finish(step - LAG)

        return carry

    def own_sums(place):
        for quad, (first, count) in enumerate(spans):
            here, there = pl.ds(first, count), pl.ds(first + HALO, count)
            mines = [(own[0, mine, here], own[1, mine, here]) for mine in (0, 1)]
            for other in (0, 1):
                b_re = held[place, 0, other, here].astype(jnp.float32)
                b_im = held[place, 1, other, here].astype(jnp.float32)
                values = []
                for a_re, a_im in mines:
                    values += [a_re * b_re + a_im * b_im, a_im * b_re - a_re * b_im]
                values.append(b_re * b_re + b_im * b_im)
                for f, value in enumerate(values):
                    fields[other, f, there] = value
                    quads[other, f, quad] = jnp.sum(value, axis=0)
        ahead, ahead_second = next_offsets[0], next_offsets[1]
        sixth, seventh = last_offsets[0], last_offsets[1]
        for other in (0, 1):
            for f in range(5):
                quad = [quads[other, f, m] for m in range(rows + 1)]
                for o in range(rows):
                    window = quad[o] + quad[o + 1]
                    for k in range(3):
                        window = window + fields[other, f, outer[3 * o + k]]
                    sums[pl.ds(other * 320 + f * 64 + o * 8, 8), :] = window
                line = [fields[other, f, HALO + l] for l in range(HALO)]
                near = line[0] + line[1]
                for l in (2, 3, 4):
                    near = near + jnp.where(seventh >= l - 1, line[l], 0.0)
                single = jnp.where(sixth >= 3, line[0], 0.0)
                line = [fields[other, f, lines + l] for l in range(HALO)]
                far = line[3] + line[4]
                for l in (0, 1, 2):
                    far = far + jnp.where(ahead <= l, line[l], 0.0)
                far_second = jnp.where(ahead_second <= 0, line[4], 0.0)
                for group, value in ((80, far), (90, far_second), (104, single), (114, near)):
                    sums[pl.ds((group + other * 5 + f) * 8, 8), :] = value

        wide = jnp.concatenate([sums[pl.ds(chunk, 128, stride=CHUNKS), :] for chunk in range(CHUNKS)], axis=1)
        high = wide.astype(jnp.bfloat16)
        low = (wide - high.astype(jnp.float32)).astype(jnp.bfloat16)
        both = jnp.dot(jnp.concatenate([high, low], axis=0), box[...], preferred_element_type=jnp.float32)
        cross[place] = both[:128] + both[128:]
        to_after(place).start()
        to_before(place).start()

    sub = lax.broadcasted_iota(jnp.int32, (rows, columns), 0)
    top = jnp.logical_and(sub == 0, strip > 0)
    second = jnp.logical_and(sub == 1, strip > 0)
    next_last = jnp.logical_and(sub == rows - 2, strip < strips - 1)
    last = jnp.logical_and(sub == rows - 1, strip < strips - 1)
    indices = []
    for row, direction, distance, side in BLOCKS:
        y_ = y - distance if direction == 0 else y + distance
        indices.append(at(1 - half if row else half, y_, 1 - core if side else core))

    def finish(place):
        block = picked(place, indices)
        to_after(place).wait_recv()
        to_before(place).wait_recv()

        def whole(f):
            value = cross[place, 8 * f : 8 * f + 8]
            value = value + jnp.where(top, from_before[place, f : f + 1], 0.0)
            value = value + jnp.where(second, from_before[place, 10 + f : 11 + f], 0.0)
            value = value + jnp.where(next_last, from_after[place, f : f + 1], 0.0)
            return value + jnp.where(last, from_after[place, 10 + f : 11 + f], 0.0)

        others = [lax.rsqrt(whole(5 * other + 4) + EPSILON) for other in (0, 1)]

        @pl.when(place == 0)
        def _():
            for mine in (0, 1):
                scale[mine] = others[mine]

        for mine in (0, 1):
            mine_scale = scale[mine]
            for other in (0, 1):
                later = numbers[0, columns + block] * 2 + other > numbers[0, columns + date] * 2 + mine
                for part in (0, 1):
                    value = whole(5 * other + 2 * mine + part) * mine_scale * others[other]
                    out[part, mine, block * 2 + other] = jnp.where(later, value, 0.0)

    lax.fori_loop(0, len(BLOCKS) + LAG - FIRST, lambda n, c: one_step(n + FIRST, c), 0)

    for which in (0, 1):
        offset(which).wait_send()
        across(which).wait_send()
    for row in (0, 1):
        for distance in range(5):
            for direction in (0, 1) if distance else (0,):
                for part in parts_of(direction, distance):
                    if distance:
                        ring(row, direction, distance, part).wait_send()
                if distance < 4 or direction == 1:
                    beside(row, direction, distance).wait_send()

    def sent(place, carry):
        to_after(place).wait_send()
        to_before(place).wait_send()
        return carry

    lax.fori_loop(0, len(BLOCKS), sent, 0)


def on_device(slc, block_order, az_offset, rg_offset):
    parts, dates, lines, samples = slc.shape
    rows, columns = lines // STEP, samples // STEP
    count = block_order.shape[0]
    total = lines + 2 * HALO
    vmem = pl.BlockSpec(memory_space=pltpu.VMEM)
    dma = pltpu.SemaphoreType.DMA
    tile = (CHUNKS, 128)
    width = -(-(columns + count + rows) // 128) * 128
    spare = jnp.zeros((width - columns - count - rows,), jnp.int32)
    small = jnp.concatenate([rg_offset, block_order, az_offset, spare])[None]
    return pl.pallas_call(
        body,
        out_shape=jax.ShapeDtypeStruct((2, dates, dates * count, rows, columns), jnp.float32),
        in_specs=[vmem, vmem],
        out_specs=vmem,
        scratch_shapes=[
            pltpu.VMEM((count, 2, dates, lines, *tile), jnp.bfloat16),
            pltpu.VMEM((2, dates, lines, *tile), jnp.float32),
            pltpu.VMEM((dates, 5, total, *tile), jnp.float32),
            pltpu.VMEM((dates, 5, rows + 1, *tile), jnp.float32),
            pltpu.VMEM((128 * CHUNKS, 128), jnp.float32),
            pltpu.VMEM((samples, columns), jnp.bfloat16),
            pltpu.VMEM((dates, rows, columns), jnp.float32),
            pltpu.VMEM((count, 128, columns), jnp.float32),
            pltpu.VMEM((count, 24, columns), jnp.float32),
            pltpu.VMEM((count, 24, columns), jnp.float32),
            pltpu.SMEM((1, width), jnp.int32),
            pltpu.SMEM((3 * rows,), jnp.int32),
            pltpu.VMEM((4, 8, 128), jnp.float32),
            pltpu.VMEM((2, 8, 128), jnp.float32),
            pltpu.VMEM((2, 8, 128), jnp.float32),
            dma((2, 2, 4, 2)), dma((2, 2, 4, 2)),
            dma((2,)), dma((2,)),
            dma((count,)), dma((count,)),
            dma((2,)), dma((2,)),
            dma((2, count)), dma((2, count)),
            dma((2,)),
        ],
        compiler_params=pltpu.CompilerParams(
            collective_id=0, has_side_effects=True, vmem_limit_bytes=48 * 2**20
        ),
    )(small, slc.reshape(parts, dates, lines, *tile))


def solution(mesh):
    placed = (P(None, "date", "strip", None), P(), P("strip"), P())
    return jax.shard_map(
        on_device,
        mesh=mesh,
        in_specs=placed,
        out_specs=P(None, "date", None, "strip", None),
        check_vma=False,
    )
```

```python
import functools

import jax
import jax.numpy as jnp
from jax import lax
from jax.experimental import pallas as pl
from jax.experimental.pallas import tpu as pltpu
from jax.sharding import PartitionSpec as P

RG_WIN = 5
STEP = 4
HALO = 5
EPSILON = 1e-06
MESH = pl.DeviceIdType.MESH

CHUNKS = 8
COLUMN = 8

BLOCKS = [
    (0, 0, 0, 0), (0, 0, 0, 1),
    (0, 0, 1, 0), (0, 1, 1, 0), (0, 0, 1, 1), (0, 1, 1, 1),
    (0, 0, 2, 0), (0, 1, 2, 0), (0, 0, 2, 1), (0, 1, 2, 1),
    (1, 0, 0, 0), (1, 0, 0, 1),
    (0, 0, 3, 0), (0, 1, 3, 0), (0, 0, 3, 1), (0, 1, 3, 1),
    (1, 0, 1, 0), (1, 1, 1, 0), (1, 0, 1, 1), (1, 1, 1, 1),
    (0, 0, 4, 0), (0, 0, 4, 1),
    (1, 0, 2, 0), (1, 1, 2, 0), (1, 0, 2, 1), (1, 1, 2, 1),
    (1, 0, 3, 0), (1, 1, 3, 0), (1, 0, 3, 1), (1, 1, 3, 1),
    (1, 0, 4, 0), (1, 0, 4, 1),
]
SLOT = {block: place for place, block in enumerate(BLOCKS)}
FIRST = -3
LAG = 10
EVENTS = {
    -3: [("ring", 0, 1, 0)],
    -2: [("ring", 0, 1, 1)],
    0: [("offsets",)],
    1: [("across", 0)],
    2: [("ring", 0, 2, 0)],
    3: [("ring", 0, 2, 1)],
    5: [("across", 1)],
    7: [("ring", 1, 1, 0)],
    9: [("ring", 0, 3, 0)],
    11: [("ring", 0, 3, 1)],
    13: [("ring", 1, 1, 1)],
    15: [("ring", 1, 2, 0)],
    18: [("ring", 0, 4, 0)],
    20: [("ring", 1, 2, 1)],
    23: [("ring", 1, 3, 0)],
    25: [("ring", 1, 3, 1)],
    29: [("ring", 1, 4, 0)],
}
for place, (row, direction, distance, sibling) in enumerate(BLOCKS):
    if sibling:
        EVENTS.setdefault(place, []).append(("beside", row, direction, distance))


def slot_of(row, direction, distance, sibling=0):
    return SLOT[(row, direction if 0 < distance < 4 else 0, distance, sibling)]


def picked(place, values):
    while len(values) > 1:
        odd = place % 2 == 1
        values = [jnp.where(odd, high, low) for low, high in zip(values[::2], values[1::2])]
        place = place // 2
    return values[0]


def body(
    small, x, out,
    held, own, fields, quads, sums, box, scale, cross, from_before, from_after,
    numbers, outer, my_offsets, next_offsets, last_offsets,
    ring_send, ring_recv, across_send, across_recv, sib_send, sib_recv, offset_send, offset_recv,
    part_send, part_recv, local_sem,
):
    date, strip = lax.axis_index("date"), lax.axis_index("strip")
    strips = lax.axis_size("strip")
    core, y, half = date % 2, (date // 2) % COLUMN, date // (2 * COLUMN)
    lines = x.shape[2]
    rows, columns = lines // STEP, box.shape[1]
    first_az = columns + len(BLOCKS)

    def at(half_, y_, core_):
        return half_ * (2 * COLUMN) + ((y_ + COLUMN) % COLUMN) * 2 + core_

    upper, lower = (at(half, y + 1, core), strip), (at(half, y - 1, core), strip)
    facing, sibling = (at(1 - half, y, core), strip), (at(half, y, 1 - core), strip)
    after = (date, (strip + 1) % strips)
    before = (date, (strip + strips - 1) % strips)

    to_scalars = pltpu.make_async_copy(small, numbers, local_sem.at[1])
    to_scalars.start()
    barrier = pltpu.get_barrier_semaphore()
    for target in (upper, lower, facing, sibling, after, before):
        pl.semaphore_signal(barrier, inc=1, device_id=target, device_id_type=MESH)
    pl.semaphore_wait(barrier, 6)

    def copy(src, dst, send, recv, target):
        return pltpu.make_async_remote_copy(
            src_ref=src, dst_ref=dst, send_sem=send, recv_sem=recv, device_id=target, device_id_type=MESH
        )

    def offset(which):
        send, recv = offset_send.at[which], offset_recv.at[which]
        if which == 0:
            return copy(my_offsets.at[pl.ds(2, 2)], last_offsets, send, recv, after)
        return copy(my_offsets.at[pl.ds(0, 2)], next_offsets, send, recv, before)

    def source_of(row, direction, distance, part):
        if row == 0 and distance == 0:
            return x.at[part]
        return held.at[slot_of(row, direction, distance), part]

    def ring(row, direction, distance, part):
        target = upper if direction == 0 else lower
        index = (row, direction, distance - 1, part)
        return copy(
            source_of(row, direction, distance - 1, part), held.at[slot_of(row, direction, distance), part],
            ring_send.at[index], ring_recv.at[index], target,
        )

    def across(part):
        return copy(
            x.at[part], held.at[slot_of(1, 0, 0), part], across_send.at[part], across_recv.at[part], facing
        )

    def beside(row, direction, distance):
        place = slot_of(row, direction, distance, 1)
        source = x if row == 0 and distance == 0 else held.at[slot_of(row, direction, distance)]
        return copy(source, held.at[place], sib_send.at[place], sib_recv.at[place], sibling)

    def to_after(place):
        return copy(
            cross.at[place, pl.ds(80, 24)], from_before.at[place], part_send.at[0, place], part_recv.at[0, place],
            after,
        )

    def to_before(place):
        return copy(
            cross.at[place, pl.ds(104, 24)], from_after.at[place], part_send.at[1, place], part_recv.at[1, place],
            before,
        )

    def parts_of(direction, distance):
        return (0, 1) if distance < 4 else (direction,)

    local = pltpu.make_async_copy(x, held.at[0], local_sem.at[0])

    def event(kind, *what):
        if kind == "offsets":
            offset(0).wait_recv()
            offset(1).wait_recv()
            local.wait()
        elif kind == "across":
            (part,) = what
            across(part).wait_recv()
            for direction in (0, 1):
                ring(1, direction, 1, part).start()
            if part == 1:
                beside(1, 0, 0).start()
        elif kind == "ring":
            row, distance, part = what
            for direction in (0, 1):
                if distance == 4:
                    part = direction
                ring(row, direction, distance, part).wait_recv()
                if distance < 4 and part in parts_of(direction, distance + 1):
                    ring(row, direction, distance + 1, part).start()
                if part == 1 and (distance < 4 or direction == 1):
                    beside(row, direction, distance).start()
        else:
            beside(*what).wait_recv()

    for part in (0, 1):
        for direction in (0, 1):
            ring(0, direction, 1, part).start()
        across(part).start()
    local.start()
    beside(0, 0, 0).start()
    to_scalars.wait()

    def az_offset(o):
        return numbers[0, first_az + o]

    for which, o in enumerate((0, 1, rows - 2, rows - 1)):
        my_offsets[which] = jnp.full((8, 128), az_offset(o), jnp.int32).astype(jnp.float32)
    offset(0).start()
    offset(1).start()

    sample = lax.broadcasted_iota(jnp.int32, (128, columns), 0)
    centre = STEP * lax.broadcasted_iota(jnp.int32, (128, columns), 1) + small[:, :columns]
    for chunk in range(CHUNKS):
        inside = jnp.abs(sample + 128 * chunk - centre) <= RG_WIN // 2
        box[pl.ds(128 * chunk, 128), :] = jnp.where(inside, 1.0, 0.0).astype(jnp.bfloat16)
    nothing = jnp.zeros((HALO, CHUNKS, 128), jnp.float32)
    for other in (0, 1):
        for f in range(5):
            fields[other, f, 0:HALO] = nothing
            fields[other, f, lines + HALO :] = nothing
    spans = [(0, 2)] + [(first, 4) for first in range(2, lines - 2, 4)] + [(lines - 2, 2)]
    for o in range(rows):
        for k in range(3):
            outer[3 * o + k] = STEP * o + k + jnp.where(az_offset(o) > k, 2 * HALO + 1, 0)
    sums[80 * 8 :, :] = jnp.zeros((48 * 8, 128), jnp.float32)
    for part in (0, 1):
        for mine in (0, 1):
            own[part, mine] = x[part, mine].astype(jnp.float32)

    def steps(step, low, high):
        here = [place for place in EVENTS if low <= place < high]
        if high - low == 1 or not here:
            for place in here:
                for one in EVENTS[place]:
                    event(*one)
            return
        middle = (low + high) // 2

        @pl.when(step < middle)
        def _():
            steps(step, low, middle)

        @pl.when(step >= middle)
        def _():
            steps(step, middle, high)

    def one_step(step, carry):
        @pl.when(step < len(BLOCKS))
        def _():
            steps(step, FIRST, len(BLOCKS))

        @pl.when(jnp.logical_and(step >= 0, step < len(BLOCKS)))
        def _():
            own_sums(step)

        @pl.when(step >= LAG)
        def _():
            finish(step - LAG)

        return carry

    def own_sums(place):
        for quad, (first, count) in enumerate(spans):
            here, there = pl.ds(first, count), pl.ds(first + HALO, count)
            mines = [(own[0, mine, here], own[1, mine, here]) for mine in (0, 1)]
            for other in (0, 1):
                b_re = held[place, 0, other, here].astype(jnp.float32)
                b_im = held[place, 1, other, here].astype(jnp.float32)
                values = []
                for a_re, a_im in mines:
                    values += [a_re * b_re + a_im * b_im, a_im * b_re - a_re * b_im]
                values.append(b_re * b_re + b_im * b_im)
                for f, value in enumerate(values):
                    fields[other, f, there] = value
                    quads[other, f, quad] = jnp.sum(value, axis=0)
        ahead, ahead_second = next_offsets[0], next_offsets[1]
        sixth, seventh = last_offsets[0], last_offsets[1]
        for other in (0, 1):
            for f in range(5):
                quad = [quads[other, f, m] for m in range(rows + 1)]
                for o in range(rows):
                    window = quad[o] + quad[o + 1]
                    for k in range(3):
                        window = window + fields[other, f, outer[3 * o + k]]
                    sums[pl.ds(other * 320 + f * 64 + o * 8, 8), :] = window
                line = [fields[other, f, HALO + l] for l in range(HALO)]
                near = line[0] + line[1]
                for l in (2, 3, 4):
                    near = near + jnp.where(seventh >= l - 1, line[l], 0.0)
                single = jnp.where(sixth >= 3, line[0], 0.0)
                line = [fields[other, f, lines + l] for l in range(HALO)]
                far = line[3] + line[4]
                for l in (0, 1, 2):
                    far = far + jnp.where(ahead <= l, line[l], 0.0)
                far_second = jnp.where(ahead_second <= 0, line[4], 0.0)
                for group, value in ((80, far), (90, far_second), (104, single), (114, near)):
                    sums[pl.ds((group + other * 5 + f) * 8, 8), :] = value

        wide = jnp.concatenate([sums[pl.ds(chunk, 128, stride=CHUNKS), :] for chunk in range(CHUNKS)], axis=1)
        high = wide.astype(jnp.bfloat16)
        low = (wide - high.astype(jnp.float32)).astype(jnp.bfloat16)
        both = jnp.dot(jnp.concatenate([high, low], axis=0), box[...], preferred_element_type=jnp.float32)
        cross[place] = both[:128] + both[128:]
        to_after(place).start()
        to_before(place).start()

    sub = lax.broadcasted_iota(jnp.int32, (rows, columns), 0)
    top = jnp.logical_and(sub == 0, strip > 0)
    second = jnp.logical_and(sub == 1, strip > 0)
    next_last = jnp.logical_and(sub == rows - 2, strip < strips - 1)
    last = jnp.logical_and(sub == rows - 1, strip < strips - 1)
    indices = []
    for row, direction, distance, side in BLOCKS:
        y_ = y - distance if direction == 0 else y + distance
        indices.append(at(1 - half if row else half, y_, 1 - core if side else core))

    def finish(place):
        block = picked(place, indices)
        to_after(place).wait_recv()
        to_before(place).wait_recv()

        def whole(f):
            value = cross[place, 8 * f : 8 * f + 8]
            value = value + jnp.where(top, from_before[place, f : f + 1], 0.0)
            value = value + jnp.where(second, from_before[place, 10 + f : 11 + f], 0.0)
            value = value + jnp.where(next_last, from_after[place, f : f + 1], 0.0)
            return value + jnp.where(last, from_after[place, 10 + f : 11 + f], 0.0)

        others = [lax.rsqrt(whole(5 * other + 4) + EPSILON) for other in (0, 1)]

        @pl.when(place == 0)
        def _():
            for mine in (0, 1):
                scale[mine] = others[mine]

        for mine in (0, 1):
            mine_scale = scale[mine]
            for other in (0, 1):
                later = numbers[0, columns + block] * 2 + other > numbers[0, columns + date] * 2 + mine
                for part in (0, 1):
                    value = whole(5 * other + 2 * mine + part) * mine_scale * others[other]
                    out[part, mine, block * 2 + other] = jnp.where(later, value, 0.0)

    lax.fori_loop(0, len(BLOCKS) + LAG - FIRST, lambda n, c: one_step(n + FIRST, c), 0)

    for which in (0, 1):
        offset(which).wait_send()
        across(which).wait_send()
    for row in (0, 1):
        for distance in range(5):
            for direction in (0, 1) if distance else (0,):
                for part in parts_of(direction, distance):
                    if distance:
                        ring(row, direction, distance, part).wait_send()
                if distance < 4 or direction == 1:
                    beside(row, direction, distance).wait_send()

    def sent(place, carry):
        to_after(place).wait_send()
        to_before(place).wait_send()
        return carry

    lax.fori_loop(0, len(BLOCKS), sent, 0)


def on_device(slc, block_order, az_offset, rg_offset):
    parts, dates, lines, samples = slc.shape
    rows, columns = lines // STEP, samples // STEP
    count = block_order.shape[0]
    total = lines + 2 * HALO
    vmem = pl.BlockSpec(memory_space=pltpu.VMEM)
    dma = pltpu.SemaphoreType.DMA
    tile = (CHUNKS, 128)
    width = -(-(columns + count + rows) // 128) * 128
    spare = jnp.zeros((width - columns - count - rows,), jnp.int32)
    small = jnp.concatenate([rg_offset, block_order, az_offset, spare])[None]
    return pl.pallas_call(
        body,
        out_shape=jax.ShapeDtypeStruct((2, dates, dates * count, rows, columns), jnp.float32),
        in_specs=[vmem, vmem],
        out_specs=vmem,
        scratch_shapes=[
            pltpu.VMEM((count, 2, dates, lines, *tile), jnp.bfloat16),
            pltpu.VMEM((2, dates, lines, *tile), jnp.float32),
            pltpu.VMEM((dates, 5, total, *tile), jnp.float32),
            pltpu.VMEM((dates, 5, rows + 1, *tile), jnp.float32),
            pltpu.VMEM((128 * CHUNKS, 128), jnp.float32),
            pltpu.VMEM((samples, columns), jnp.bfloat16),
            pltpu.VMEM((dates, rows, columns), jnp.float32),
            pltpu.VMEM((count, 128, columns), jnp.float32),
            pltpu.VMEM((count, 24, columns), jnp.float32),
            pltpu.VMEM((count, 24, columns), jnp.float32),
            pltpu.SMEM((1, width), jnp.int32),
            pltpu.SMEM((3 * rows,), jnp.int32),
            pltpu.VMEM((4, 8, 128), jnp.float32),
            pltpu.VMEM((2, 8, 128), jnp.float32),
            pltpu.VMEM((2, 8, 128), jnp.float32),
            dma((2, 2, 4, 2)), dma((2, 2, 4, 2)),
            dma((2,)), dma((2,)),
            dma((count,)), dma((count,)),
            dma((2,)), dma((2,)),
            dma((2, count)), dma((2, count)),
            dma((2,)),
        ],
        compiler_params=pltpu.CompilerParams(
            collective_id=0, has_side_effects=True, vmem_limit_bytes=48 * 2**20
        ),
    )(small, slc.reshape(parts, dates, lines, *tile))


def solution(mesh):
    placed = (P(None, "date", "strip", None), P(), P("strip"), P())
    return jax.shard_map(
        on_device,
        mesh=mesh,
        in_specs=placed,
        out_specs=P(None, "date", None, "strip", None),
        check_vma=False,
    )
```

```python
import functools

import jax
import jax.numpy as jnp
from jax import lax
from jax.experimental import pallas as pl
from jax.experimental.pallas import tpu as pltpu
from jax.sharding import PartitionSpec as P

RG_WIN = 5
STEP = 4
HALO = 5
EPSILON = 1e-06
MESH = pl.DeviceIdType.MESH

CHUNKS = 8
COLUMN = 8

BLOCKS = [
    (0, 0, 0, 0), (0, 0, 0, 1),
    (0, 0, 1, 0), (0, 1, 1, 0), (0, 0, 1, 1), (0, 1, 1, 1),
    (0, 0, 2, 0), (0, 1, 2, 0), (0, 0, 2, 1), (0, 1, 2, 1),
    (1, 0, 0, 0), (1, 0, 0, 1),
    (0, 0, 3, 0), (0, 1, 3, 0), (0, 0, 3, 1), (0, 1, 3, 1),
    (1, 0, 1, 0), (1, 1, 1, 0), (1, 0, 1, 1), (1, 1, 1, 1),
    (0, 0, 4, 0), (0, 0, 4, 1),
    (1, 0, 2, 0), (1, 1, 2, 0), (1, 0, 2, 1), (1, 1, 2, 1),
    (1, 0, 3, 0), (1, 1, 3, 0), (1, 0, 3, 1), (1, 1, 3, 1),
    (1, 0, 4, 0), (1, 0, 4, 1),
]
SLOT = {block: place for place, block in enumerate(BLOCKS)}
FIRST = -4
LAG = 10
EVENTS = {
    -4: [("ring", 0, 1, 0)],
    -3: [("ring", 0, 1, 1)],
    -1: [("offsets",)],
    0: [("across", 0)],
    1: [("ring", 0, 2, 0)],
    2: [("ring", 0, 2, 1)],
    4: [("across", 1)],
    6: [("ring", 1, 1, 0)],
    8: [("ring", 0, 3, 0)],
    10: [("ring", 0, 3, 1)],
    12: [("ring", 1, 1, 1)],
    14: [("ring", 1, 2, 0)],
    17: [("ring", 0, 4, 0)],
    19: [("ring", 1, 2, 1)],
    22: [("ring", 1, 3, 0)],
    24: [("ring", 1, 3, 1)],
    28: [("ring", 1, 4, 0)],
}
for place, (row, direction, distance, sibling) in enumerate(BLOCKS):
    if sibling:
        EVENTS.setdefault(place, []).append(("beside", row, direction, distance))


def slot_of(row, direction, distance, sibling=0):
    return SLOT[(row, direction if 0 < distance < 4 else 0, distance, sibling)]


def picked(place, values):
    while len(values) > 1:
        odd = place % 2 == 1
        values = [jnp.where(odd, high, low) for low, high in zip(values[::2], values[1::2])]
        place = place // 2
    return values[0]


def body(
    small, x, out,
    held, own, fields, quads, sums, box, scale, cross, from_before, from_after,
    numbers, outer, my_offsets, next_offsets, last_offsets,
    ring_send, ring_recv, across_send, across_recv, sib_send, sib_recv, offset_send, offset_recv,
    part_send, part_recv, local_sem,
):
    date, strip = lax.axis_index("date"), lax.axis_index("strip")
    strips = lax.axis_size("strip")
    core, y, half = date % 2, (date // 2) % COLUMN, date // (2 * COLUMN)
    lines = x.shape[2]
    rows, columns = lines // STEP, box.shape[1]
    first_az = columns + len(BLOCKS)

    def at(half_, y_, core_):
        return half_ * (2 * COLUMN) + ((y_ + COLUMN) % COLUMN) * 2 + core_

    upper, lower = (at(half, y + 1, core), strip), (at(half, y - 1, core), strip)
    facing, sibling = (at(1 - half, y, core), strip), (at(half, y, 1 - core), strip)
    after = (date, (strip + 1) % strips)
    before = (date, (strip + strips - 1) % strips)

    to_scalars = pltpu.make_async_copy(small, numbers, local_sem.at[1])
    to_scalars.start()
    barrier = pltpu.get_barrier_semaphore()
    for target in (upper, lower, facing, sibling, after, before):
        pl.semaphore_signal(barrier, inc=1, device_id=target, device_id_type=MESH)
    pl.semaphore_wait(barrier, 6)

    def copy(src, dst, send, recv, target):
        return pltpu.make_async_remote_copy(
            src_ref=src, dst_ref=dst, send_sem=send, recv_sem=recv, device_id=target, device_id_type=MESH
        )

    def offset(which):
        send, recv = offset_send.at[which], offset_recv.at[which]
        if which == 0:
            return copy(my_offsets.at[pl.ds(2, 2)], last_offsets, send, recv, after)
        return copy(my_offsets.at[pl.ds(0, 2)], next_offsets, send, recv, before)

    def source_of(row, direction, distance, part):
        if row == 0 and distance == 0:
            return x.at[part]
        return held.at[slot_of(row, direction, distance), part]

    def ring(row, direction, distance, part):
        target = upper if direction == 0 else lower
        index = (row, direction, distance - 1, part)
        return copy(
            source_of(row, direction, distance - 1, part), held.at[slot_of(row, direction, distance), part],
            ring_send.at[index], ring_recv.at[index], target,
        )

    def across(part):
        return copy(
            x.at[part], held.at[slot_of(1, 0, 0), part], across_send.at[part], across_recv.at[part], facing
        )

    def beside(row, direction, distance):
        place = slot_of(row, direction, distance, 1)
        source = x if row == 0 and distance == 0 else held.at[slot_of(row, direction, distance)]
        return copy(source, held.at[place], sib_send.at[place], sib_recv.at[place], sibling)

    def to_after(place):
        return copy(
            cross.at[place, pl.ds(80, 24)], from_before.at[place], part_send.at[0, place], part_recv.at[0, place],
            after,
        )

    def to_before(place):
        return copy(
            cross.at[place, pl.ds(104, 24)], from_after.at[place], part_send.at[1, place], part_recv.at[1, place],
            before,
        )

    def parts_of(direction, distance):
        return (0, 1) if distance < 4 else (direction,)

    local = pltpu.make_async_copy(x, held.at[0], local_sem.at[0])

    def event(kind, *what):
        if kind == "offsets":
            offset(0).wait_recv()
            offset(1).wait_recv()
            local.wait()
        elif kind == "across":
            (part,) = what
            across(part).wait_recv()
            for direction in (0, 1):
                ring(1, direction, 1, part).start()
            if part == 1:
                beside(1, 0, 0).start()
        elif kind == "ring":
            row, distance, part = what
            for direction in (0, 1):
                if distance == 4:
                    part = direction
                ring(row, direction, distance, part).wait_recv()
                if distance < 4 and part in parts_of(direction, distance + 1):
                    ring(row, direction, distance + 1, part).start()
                if part == 1 and (distance < 4 or direction == 1):
                    beside(row, direction, distance).start()
        else:
            beside(*what).wait_recv()

    for part in (0, 1):
        for direction in (0, 1):
            ring(0, direction, 1, part).start()
        across(part).start()
    local.start()
    beside(0, 0, 0).start()
    to_scalars.wait()

    def az_offset(o):
        return numbers[0, first_az + o]

    for which, o in enumerate((0, 1, rows - 2, rows - 1)):
        my_offsets[which] = jnp.full((8, 128), az_offset(o), jnp.int32).astype(jnp.float32)
    offset(0).start()
    offset(1).start()

    sample = lax.broadcasted_iota(jnp.int32, (128, columns), 0)
    centre = STEP * lax.broadcasted_iota(jnp.int32, (128, columns), 1) + small[:, :columns]
    for chunk in range(CHUNKS):
        inside = jnp.abs(sample + 128 * chunk - centre) <= RG_WIN // 2
        box[pl.ds(128 * chunk, 128), :] = jnp.where(inside, 1.0, 0.0).astype(jnp.bfloat16)
    nothing = jnp.zeros((HALO, CHUNKS, 128), jnp.float32)
    for other in (0, 1):
        for f in range(5):
            fields[other, f, 0:HALO] = nothing
            fields[other, f, lines + HALO :] = nothing
    spans = [(0, 2)] + [(first, 4) for first in range(2, lines - 2, 4)] + [(lines - 2, 2)]
    for o in range(rows):
        for k in range(3):
            outer[3 * o + k] = STEP * o + k + jnp.where(az_offset(o) > k, 2 * HALO + 1, 0)
    sums[80 * 8 :, :] = jnp.zeros((48 * 8, 128), jnp.float32)
    for part in (0, 1):
        for mine in (0, 1):
            own[part, mine] = x[part, mine].astype(jnp.float32)

    def steps(step, low, high):
        here = [place for place in EVENTS if low <= place < high]
        if high - low == 1 or not here:
            for place in here:
                for one in EVENTS[place]:
                    event(*one)
            return
        middle = (low + high) // 2

        @pl.when(step < middle)
        def _():
            steps(step, low, middle)

        @pl.when(step >= middle)
        def _():
            steps(step, middle, high)

    def one_step(step, carry):
        @pl.when(step < len(BLOCKS))
        def _():
            steps(step, FIRST, len(BLOCKS))

        @pl.when(jnp.logical_and(step >= 0, step < len(BLOCKS)))
        def _():
            own_sums(step)

        @pl.when(step >= LAG)
        def _():
            finish(step - LAG)

        return carry

    def own_sums(place):
        for quad, (first, count) in enumerate(spans):
            here, there = pl.ds(first, count), pl.ds(first + HALO, count)
            mines = [(own[0, mine, here], own[1, mine, here]) for mine in (0, 1)]
            for other in (0, 1):
                b_re = held[place, 0, other, here].astype(jnp.float32)
                b_im = held[place, 1, other, here].astype(jnp.float32)
                values = []
                for a_re, a_im in mines:
                    values += [a_re * b_re + a_im * b_im, a_im * b_re - a_re * b_im]
                values.append(b_re * b_re + b_im * b_im)
                for f, value in enumerate(values):
                    fields[other, f, there] = value
                    quads[other, f, quad] = jnp.sum(value, axis=0)
        ahead, ahead_second = next_offsets[0], next_offsets[1]
        sixth, seventh = last_offsets[0], last_offsets[1]
        for other in (0, 1):
            for f in range(5):
                quad = [quads[other, f, m] for m in range(rows + 1)]
                for o in range(rows):
                    window = quad[o] + quad[o + 1]
                    for k in range(3):
                        window = window + fields[other, f, outer[3 * o + k]]
                    sums[pl.ds(other * 320 + f * 64 + o * 8, 8), :] = window
                line = [fields[other, f, HALO + l] for l in range(HALO)]
                near = line[0] + line[1]
                for l in (2, 3, 4):
                    near = near + jnp.where(seventh >= l - 1, line[l], 0.0)
                single = jnp.where(sixth >= 3, line[0], 0.0)
                line = [fields[other, f, lines + l] for l in range(HALO)]
                far = line[3] + line[4]
                for l in (0, 1, 2):
                    far = far + jnp.where(ahead <= l, line[l], 0.0)
                far_second = jnp.where(ahead_second <= 0, line[4], 0.0)
                for group, value in ((80, far), (90, far_second), (104, single), (114, near)):
                    sums[pl.ds((group + other * 5 + f) * 8, 8), :] = value

        wide = jnp.concatenate([sums[pl.ds(chunk, 128, stride=CHUNKS), :] for chunk in range(CHUNKS)], axis=1)
        high = wide.astype(jnp.bfloat16)
        low = (wide - high.astype(jnp.float32)).astype(jnp.bfloat16)
        both = jnp.dot(jnp.concatenate([high, low], axis=0), box[...], preferred_element_type=jnp.float32)
        cross[place] = both[:128] + both[128:]
        to_after(place).start()
        to_before(place).start()

    sub = lax.broadcasted_iota(jnp.int32, (rows, columns), 0)
    top = jnp.logical_and(sub == 0, strip > 0)
    second = jnp.logical_and(sub == 1, strip > 0)
    next_last = jnp.logical_and(sub == rows - 2, strip < strips - 1)
    last = jnp.logical_and(sub == rows - 1, strip < strips - 1)
    indices = []
    for row, direction, distance, side in BLOCKS:
        y_ = y - distance if direction == 0 else y + distance
        indices.append(at(1 - half if row else half, y_, 1 - core if side else core))

    def finish(place):
        block = picked(place, indices)
        to_after(place).wait_recv()
        to_before(place).wait_recv()

        def whole(f):
            value = cross[place, 8 * f : 8 * f + 8]
            value = value + jnp.where(top, from_before[place, f : f + 1], 0.0)
            value = value + jnp.where(second, from_before[place, 10 + f : 11 + f], 0.0)
            value = value + jnp.where(next_last, from_after[place, f : f + 1], 0.0)
            return value + jnp.where(last, from_after[place, 10 + f : 11 + f], 0.0)

        others = [lax.rsqrt(whole(5 * other + 4) + EPSILON) for other in (0, 1)]

        @pl.when(place == 0)
        def _():
            for mine in (0, 1):
                scale[mine] = others[mine]

        for mine in (0, 1):
            mine_scale = scale[mine]
            for other in (0, 1):
                later = numbers[0, columns + block] * 2 + other > numbers[0, columns + date] * 2 + mine
                for part in (0, 1):
                    value = whole(5 * other + 2 * mine + part) * mine_scale * others[other]
                    out[part, mine, block * 2 + other] = jnp.where(later, value, 0.0)

    lax.fori_loop(0, len(BLOCKS) + LAG - FIRST, lambda n, c: one_step(n + FIRST, c), 0)

    for which in (0, 1):
        offset(which).wait_send()
        across(which).wait_send()
    for row in (0, 1):
        for distance in range(5):
            for direction in (0, 1) if distance else (0,):
                for part in parts_of(direction, distance):
                    if distance:
                        ring(row, direction, distance, part).wait_send()
                if distance < 4 or direction == 1:
                    beside(row, direction, distance).wait_send()

    def sent(place, carry):
        to_after(place).wait_send()
        to_before(place).wait_send()
        return carry

    lax.fori_loop(0, len(BLOCKS), sent, 0)


def on_device(slc, block_order, az_offset, rg_offset):
    parts, dates, lines, samples = slc.shape
    rows, columns = lines // STEP, samples // STEP
    count = block_order.shape[0]
    total = lines + 2 * HALO
    vmem = pl.BlockSpec(memory_space=pltpu.VMEM)
    dma = pltpu.SemaphoreType.DMA
    tile = (CHUNKS, 128)
    width = -(-(columns + count + rows) // 128) * 128
    spare = jnp.zeros((width - columns - count - rows,), jnp.int32)
    small = jnp.concatenate([rg_offset, block_order, az_offset, spare])[None]
    return pl.pallas_call(
        body,
        out_shape=jax.ShapeDtypeStruct((2, dates, dates * count, rows, columns), jnp.float32),
        in_specs=[vmem, vmem],
        out_specs=vmem,
        scratch_shapes=[
            pltpu.VMEM((count, 2, dates, lines, *tile), jnp.bfloat16),
            pltpu.VMEM((2, dates, lines, *tile), jnp.float32),
            pltpu.VMEM((dates, 5, total, *tile), jnp.float32),
            pltpu.VMEM((dates, 5, rows + 1, *tile), jnp.float32),
            pltpu.VMEM((128 * CHUNKS, 128), jnp.float32),
            pltpu.VMEM((samples, columns), jnp.bfloat16),
            pltpu.VMEM((dates, rows, columns), jnp.float32),
            pltpu.VMEM((count, 128, columns), jnp.float32),
            pltpu.VMEM((count, 24, columns), jnp.float32),
            pltpu.VMEM((count, 24, columns), jnp.float32),
            pltpu.SMEM((1, width), jnp.int32),
            pltpu.SMEM((3 * rows,), jnp.int32),
            pltpu.VMEM((4, 8, 128), jnp.float32),
            pltpu.VMEM((2, 8, 128), jnp.float32),
            pltpu.VMEM((2, 8, 128), jnp.float32),
            dma((2, 2, 4, 2)), dma((2, 2, 4, 2)),
            dma((2,)), dma((2,)),
            dma((count,)), dma((count,)),
            dma((2,)), dma((2,)),
            dma((2, count)), dma((2, count)),
            dma((2,)),
        ],
        compiler_params=pltpu.CompilerParams(
            collective_id=0, has_side_effects=True, vmem_limit_bytes=48 * 2**20
        ),
    )(small, slc.reshape(parts, dates, lines, *tile))


def solution(mesh):
    placed = (P(None, "date", "strip", None), P(), P("strip"), P())
    return jax.shard_map(
        on_device,
        mesh=mesh,
        in_specs=placed,
        out_specs=P(None, "date", None, "strip", None),
        check_vma=False,
    )
```
